32 devices in a mesh: group: 4 (over y, core), freq: 8 (over z, x).
Axes of the slice: x: 2, y: 2, z: 4, core: 2. Of those that a mesh axis runs over, the one named last changes fastest.
Arguments:
- spectra: bfloat16 [2048, 2, 16], P('freq', None, 'group'), may hold values from -6 to 6
- templates: bfloat16 [2048, 2, 2560], P('freq', None, 'group'), may hold values from -600 to 600
- valid_start: int32 [16], replicated, may hold values from 0 to 2048
Outputs:
- peaks: float32 [2560, 16], P('group')
The draws below stay inside these ranges and needn't reach their ends.
All inputs are finite; a program needn't handle non-finite values.
Results may differ from the reference program's by a relative error of at most 0.0019.
Values may be sent and summed in bfloat16 or wider, within the bound.
A program may use at most 256 MiB of HBM per device.

```python
import math
import jax
import jax.numpy as jnp
from jax import lax

N = 4096
K = 2048
VALID = 2048
SEG = 16
TEMPLATES = 2560


def draw_templates(key, part):
    base_key, row_key, col_key = jax.random.split(jax.random.fold_in(key, 11), 3)
    base = jnp.clip(jax.random.normal(base_key, (K, 2, TEMPLATES), jnp.float32), -6.0, 6.0)
    row_scale = jnp.exp(jax.random.uniform(row_key, (TEMPLATES,), jnp.float32, 0.0, math.log(10.0)))
    col_scale = jnp.exp(jax.random.uniform(col_key, (K,), jnp.float32, 0.0, math.log(10.0)))
    return (base * row_scale[None, None, :] * col_scale[:, None, None]).astype(jnp.bfloat16)


def with_ends(values, own_key, smallest, top_value):
    spot = [jax.random.randint(jax.random.fold_in(own_key, axis), (), 0, length) for axis, length in enumerate(values.shape)]
    widest = values.shape.index(max(values.shape))
    beside = spot[:widest] + [(spot[widest] + 1) % values.shape[widest]] + spot[widest + 1:]
    return values.at[tuple(spot)].set(smallest).at[tuple(beside)].set(top_value)


def steps_of(own_key, extent, cuts, smallest, high):
    factor_of = 1.0
    for position, blocks in cuts:
        heights = jax.random.uniform(jax.random.fold_in(jax.random.fold_in(own_key, 6), position), (blocks,), jnp.float32, smallest / len(cuts), high / len(cuts))
        factor_of = factor_of * jnp.repeat(jnp.exp(heights), extent[position] // blocks).reshape((-1,) + (1,) * (len(extent) - 1 - position))
    return factor_of


def noise(own_key, shape, deviation, most, cuts=(), kind=jnp.bfloat16):
    array = jax.random.normal(own_key, shape, jnp.float32) * deviation
    if len(cuts) > 0:
        array = steps_of(own_key, shape, cuts, -0.22, 0.18) * array
    return jnp.clip(array, min=-most, max=most).astype(kind)


def setup_inputs(seed: int = 0) -> dict:
    seeds = jax.random.split(jax.random.key(seed), 4)
    return {
        "spectra": noise(seeds[0], (K, 2, SEG), 1.0, 6.0, ((0, 8), (2, 4))),
        "templates": draw_templates(jax.random.fold_in(seeds[3], 71), 0),
        "valid_start": with_ends(jax.random.randint(seeds[2], (SEG,), 0, N - VALID + 1), jax.random.fold_in(seeds[2], 1), 0, N - VALID).astype(jnp.int32),
    }


def reference(spectra, templates, valid_start):
    bank = jnp.transpose(templates, (1, 2, 0)).astype(jnp.float32)
    strain_all = jnp.transpose(spectra, (1, 2, 0))
    template_norm = jnp.sum(bank[0] * bank[0] + bank[1] * bank[1], axis=1)
    bins_index = jnp.arange(K, dtype=jnp.int32)
    lag_index = jnp.arange(N, dtype=jnp.int32)
    angle = ((bins_index[:, None] * lag_index[None, :]) % N).astype(jnp.float32) * (2.0 * math.pi / N)
    cosine = jnp.cos(angle)
    sine_part = jnp.sin(angle)
    table = jnp.concatenate([jnp.concatenate([cosine, sine_part], 1), jnp.concatenate([-sine_part, cosine], 1)], 0).astype(jnp.bfloat16)

    def one_segment(segment):
        strain = lax.dynamic_index_in_dim(strain_all, segment, 1, False).astype(jnp.float32)
        cross_re = bank[0] * strain[0][None, :] + bank[1] * strain[1][None, :]
        cross_im = bank[0] * strain[1][None, :] - bank[1] * strain[0][None, :]
        cross = jnp.concatenate([cross_re, cross_im], 1).astype(jnp.bfloat16)
        series = jnp.dot(cross, table, preferred_element_type=jnp.float32)
        power = (series[:, :N] * series[:, :N] + series[:, N:] * series[:, N:]) / template_norm[:, None]
        first = valid_start[segment]
        inside = (lag_index >= first) & (lag_index < first + VALID)
        return jnp.max(jnp.where(inside[None, :], power, jnp.float32(0.0)), axis=1)

    peaks = lax.map(one_segment, jnp.arange(SEG, dtype=jnp.int32))
    return peaks.T
```

```python
import functools
import math

import jax
import jax.numpy as jnp
import numpy as np
from jax import lax
from jax.experimental import pallas as pl
from jax.experimental.pallas import tpu as pltpu
from jax.sharding import PartitionSpec as P

LANES = 128
RADIX = 16
SUB = 8
SCALE = 1.1328125


def rotation(angle, row_axis, col_axis):
    cosine, sine = np.cos(angle), np.sin(angle)
    top = np.stack([cosine, -sine], col_axis)
    bottom = np.stack([sine, cosine], col_axis)
    return np.stack([top, bottom], row_axis)


def tables(bins):
    lags = 2 * bins
    inner = lags // RADIX
    a = np.arange(bins // RADIX)
    tau1 = np.arange(inner)
    angle = 2.0 * math.pi * ((tau1[:, None] * a[None, :]) % inner) / inner
    first = rotation(angle.reshape(inner // SUB, SUB, a.size), 1, 2)
    first = first.reshape(inner // SUB, 2, SUB, 2 * a.size)
    turn = 2.0 * math.pi * tau1.reshape(inner // SUB, SUB, 1) / lags
    turn = np.stack([np.cos(turn), np.sin(turn)], 0)
    b = np.arange(RADIX)
    angle = 2.0 * math.pi * ((b[:, None] * b[None, :]) % RADIX) / RADIX
    second = rotation(angle, 0, 2) * SCALE
    second = second.reshape(2 * RADIX, 2 * RADIX)
    second = np.kron(second, np.eye(SUB))
    return first.astype(np.float32), turn.astype(np.float32), second.astype(jnp.bfloat16)


def kernel(valid, r_ref, d_ref, base_ref, turn_ref, w2_ref, vs_ref, out_ref, work_ref, w1_ref, dexp_ref, y_ref):
    step = pl.program_id(0)
    width = out_ref.shape[2]
    parts, _, depth2, _ = r_ref.shape
    depth = depth2 // 2
    segs = d_ref.shape[3]
    per_tile = LANES // segs
    half = parts * depth
    rows2, cols2 = w2_ref.shape
    groups = y_ref.shape[0]
    inner = groups * SUB

    @pl.when(step == 0)
    def _():
        work_ref[...] = base_ref[...]

        @pl.loop(0, RADIX)
        def _(b):
            w1_ref[b] = work_ref[...].reshape(w1_ref.shape[1:]).astype(jnp.bfloat16)
            top, bottom = work_ref[:, 0], work_ref[:, 1]
            cosine, sine = turn_ref[0], turn_ref[1]
            work_ref[:, 0] = top * cosine - bottom * sine
            work_ref[:, 1] = bottom * cosine + top * sine

        seg_spread = (
            lax.broadcasted_iota(jnp.int32, (segs, LANES), 0)
            == lax.broadcasted_iota(jnp.int32, (segs, LANES), 1) // per_tile
        ).astype(jnp.bfloat16)

        @pl.loop(0, RADIX)
        def _(b):
            piece = d_ref[:, b].reshape(2 * half, segs)
            dexp_ref[b] = jnp.dot(piece, seg_spread, preferred_element_type=jnp.float32)

    lane = lax.broadcasted_iota(jnp.int32, (LANES, width), 1)
    wanted = step * (width // segs) + (lane // LANES) * per_tile + lane % per_tile
    pick = (lax.broadcasted_iota(jnp.int32, (LANES, width), 0) == wanted).astype(jnp.bfloat16)

    def split(x):
        x = x.reshape(parts, 2, depth, x.shape[1])
        return x[:, 0].reshape(half, -1), x[:, 1].reshape(half, -1)

    def first_stage(b, norm):
        bank = jnp.dot(
            r_ref[:, b].reshape(2 * half, LANES), pick, preferred_element_type=jnp.float32
        )
        h0, h1 = split(bank)
        d0, d1 = split(dexp_ref[b])
        d0 = jnp.concatenate([d0] * (width // LANES), 1)
        d1 = jnp.concatenate([d1] * (width // LANES), 1)
        square = h0 * h0 + h1 * h1
        norm = norm + jnp.sum(square.reshape(half // SUB, SUB, width), 0)
        cross = jnp.concatenate([h0 * d0 + h1 * d1, h0 * d1 - h1 * d0], 0).astype(jnp.bfloat16)
        y = jnp.dot(w1_ref[b], cross, preferred_element_type=jnp.float32)
        y_ref[:, b] = y.astype(jnp.bfloat16).reshape(groups, 2 * SUB, width)
        return norm

    norm = lax.fori_loop(
        0, RADIX, first_stage, jnp.zeros((SUB, width), jnp.float32), unroll=2
    )
    offset = lax.broadcasted_iota(jnp.int32, (SUB, width), 0) - vs_ref[...]
    row = lax.broadcasted_iota(jnp.int32, (RADIX, SUB, width), 0) * inner

    def second_stage(g, best):
        z = jnp.dot(
            w2_ref[...], y_ref[g].reshape(cols2, width), preferred_element_type=jnp.float32
        )
        re, im = z[: rows2 // 2], z[rows2 // 2 :]
        power = (re * re + im * im).reshape(RADIX, SUB, width)
        late = row + (offset + g * SUB)[None]
        inside = (late >= 0) & (late < valid)
        return jnp.maximum(best, jnp.max(jnp.where(inside, power, 0.0), 0))

    best = lax.fori_loop(
        0, groups, second_stage, jnp.zeros((SUB, width), jnp.float32), unroll=4
    )
    norm = jnp.sum(norm, 0, keepdims=True) * (SCALE * SCALE)
    out_ref[0] = jnp.max(best, 0, keepdims=True) / norm


def correlate(received, strain, starts, rows):
    parts, _, depth2, _ = received.shape
    segs = strain.shape[3]
    bins = parts * RADIX * depth2 // 2
    base, turn, second = tables(bins)
    per_tile = LANES // segs
    tiles = -(-rows // per_tile)
    width = 2 * LANES if tiles % 2 == 0 else LANES
    steps = tiles * LANES // width
    starts = jnp.tile(jnp.repeat(starts, per_tile), width // LANES)
    starts = jnp.broadcast_to(starts[None, :], (SUB, width))
    groups = 2 * bins // RADIX // SUB
    whole = pl.BlockSpec(memory_space=pltpu.VMEM)
    out = pl.pallas_call(
        functools.partial(kernel, bins),
        grid=(steps,),
        out_shape=jax.ShapeDtypeStruct((steps, 1, width), jnp.float32),
        in_specs=[whole] * 6,
        out_specs=pl.BlockSpec((1, 1, width), lambda i: (i, 0, 0)),
        scratch_shapes=[
            pltpu.VMEM(base.shape, jnp.float32),
            pltpu.VMEM((RADIX, groups * 2 * SUB, 2 * bins // RADIX), jnp.bfloat16),
            pltpu.VMEM((RADIX, parts * depth2, LANES), jnp.float32),
            pltpu.VMEM((groups, RADIX, 2 * SUB, width), jnp.bfloat16),
        ],
        compiler_params=pltpu.CompilerParams(vmem_limit_bytes=50 * 1024 * 1024),
    )(received, strain, jnp.asarray(base), jnp.asarray(turn), jnp.asarray(second), starts)
    out = out.reshape(tiles, segs, per_tile)
    return out.transpose(0, 2, 1).reshape(tiles * per_tile, segs)[:rows]


def join_parts(pieces, depth):
    if depth % SUB == 0:
        return pieces
    parts, _, _, last = pieces.shape
    pieces = pieces.reshape(parts, RADIX, 2, depth, last).transpose(1, 2, 0, 3, 4)
    return pieces.reshape(1, RADIX, 2 * parts * depth, last)


def on_device(spectra, templates, valid_start):
    parts = lax.axis_size("freq")
    bins_here, _, rows_here = templates.shape
    depth = bins_here // RADIX
    rows = rows_here // parts
    bank = templates.reshape(depth, RADIX, 2, parts, rows).transpose(3, 1, 2, 0, 4)
    bank = jnp.pad(bank, ((0, 0),) * 4 + ((0, LANES - rows),))
    bank = bank.reshape(parts, RADIX, 2 * depth, LANES)
    received = lax.all_to_all(bank, "freq", 0, 0, tiled=True)
    strain = spectra.reshape(depth, RADIX, 2, -1).transpose(1, 2, 0, 3)
    strain = strain.reshape(RADIX, 2 * depth, -1)
    strain = lax.all_gather(strain, ("freq", "group"), axis=0)
    strain = strain.reshape((parts, -1) + strain.shape[1:])
    strain = strain.transpose(0, 2, 3, 1, 4).reshape(parts, RADIX, 2 * depth, -1)
    peaks = correlate(join_parts(received, depth), join_parts(strain, depth), valid_start, rows)
    return lax.all_gather(peaks, "freq", axis=0, tiled=True)


def solution(mesh):
    in_specs = (P("freq", None, "group"), P("freq", None, "group"), P())
    out_specs = P("group", None)
    return jax.shard_map(
        on_device, mesh=mesh, in_specs=in_specs, out_specs=out_specs, check_vma=False
    )
```

```python
import functools
import math

import jax
import jax.numpy as jnp
import numpy as np
from jax import lax
from jax.experimental import pallas as pl
from jax.experimental.pallas import tpu as pltpu
from jax.sharding import PartitionSpec as P

LANES = 128
RADIX = 16
SUB = 8
SCALE = 1.1328125


def rotation(angle, row_axis, col_axis):
    cosine, sine = np.cos(angle), np.sin(angle)
    top = np.stack([cosine, -sine], col_axis)
    bottom = np.stack([sine, cosine], col_axis)
    return np.stack([top, bottom], row_axis)


def tables(bins):
    lags = 2 * bins
    inner = lags // RADIX
    a = np.arange(bins // RADIX)
    tau1 = np.arange(inner)
    angle = 2.0 * math.pi * ((tau1[:, None] * a[None, :]) % inner) / inner
    first = rotation(angle.reshape(inner // SUB, SUB, a.size), 1, 2)
    first = first.reshape(inner // SUB, 2, SUB, 2 * a.size)
    turn = 2.0 * math.pi * tau1.reshape(inner // SUB, SUB, 1) / lags
    turn = np.stack([np.cos(turn), np.sin(turn)], 0)
    b = np.arange(RADIX)
    angle = 2.0 * math.pi * ((b[:, None] * b[None, :]) % RADIX) / RADIX
    second = rotation(angle, 0, 2) * SCALE
    second = second.reshape(2 * RADIX, 2 * RADIX)
    second = np.kron(second, np.eye(SUB))
    return first.astype(np.float32), turn.astype(np.float32), second.astype(jnp.bfloat16)


def kernel(valid, r_ref, d_ref, base_ref, turn_ref, w2_ref, vs_ref, out_ref, work_ref, w1_ref, dexp_ref, y_ref):
    step = pl.program_id(0)
    width = out_ref.shape[2]
    parts, _, depth2, _ = r_ref.shape
    depth = depth2 // 2
    segs = d_ref.shape[3]
    per_tile = LANES // segs
    half = parts * depth
    rows2, cols2 = w2_ref.shape
    groups = y_ref.shape[0]
    inner = groups * SUB

    @pl.when(step == 0)
    def _():
        work_ref[...] = base_ref[...]

        @pl.loop(0, RADIX)
        def _(b):
            w1_ref[b] = work_ref[...].reshape(w1_ref.shape[1:]).astype(jnp.bfloat16)
            top, bottom = work_ref[:, 0], work_ref[:, 1]
            cosine, sine = turn_ref[0], turn_ref[1]
            work_ref[:, 0] = top * cosine - bottom * sine
            work_ref[:, 1] = bottom * cosine + top * sine

        seg_spread = (
            lax.broadcasted_iota(jnp.int32, (segs, LANES), 0)
            == lax.broadcasted_iota(jnp.int32, (segs, LANES), 1) // per_tile
        ).astype(jnp.bfloat16)

        @pl.loop(0, RADIX)
        def _(b):
            piece = d_ref[:, b].reshape(2 * half, segs)
            dexp_ref[b] = jnp.dot(piece, seg_spread, preferred_element_type=jnp.float32)

    lane = lax.broadcasted_iota(jnp.int32, (LANES, width), 1)
    wanted = step * (width // segs) + (lane // LANES) * per_tile + lane % per_tile
    pick = (lax.broadcasted_iota(jnp.int32, (LANES, width), 0) == wanted).astype(jnp.bfloat16)

    def split(x):
        x = x.reshape(parts, 2, depth, x.shape[1])
        return x[:, 0].reshape(half, -1), x[:, 1].reshape(half, -1)

    def first_stage(b, norm):
        bank = jnp.dot(
            r_ref[:, b].reshape(2 * half, LANES), pick, preferred_element_type=jnp.float32
        )
        h0, h1 = split(bank)
        d0, d1 = split(dexp_ref[b])
        d0 = jnp.concatenate([d0] * (width // LANES), 1)
        d1 = jnp.concatenate([d1] * (width // LANES), 1)
        square = h0 * h0 + h1 * h1
        norm = norm + jnp.sum(square.reshape(half // SUB, SUB, width), 0)
        cross = jnp.concatenate([h0 * d0 + h1 * d1, h0 * d1 - h1 * d0], 0).astype(jnp.bfloat16)
        y = jnp.dot(w1_ref[b], cross, preferred_element_type=jnp.float32)
        y_ref[:, b] = y.astype(jnp.bfloat16).reshape(groups, 2 * SUB, width)
        return norm

    norm = lax.fori_loop(
        0, RADIX, first_stage, jnp.zeros((SUB, width), jnp.float32), unroll=2
    )
    offset = lax.broadcasted_iota(jnp.int32, (SUB, width), 0) - vs_ref[...]
    row = lax.broadcasted_iota(jnp.int32, (RADIX, SUB, width), 0) * inner

    def second_stage(g, best):
        z = jnp.dot(
            w2_ref[...], y_ref[g].reshape(cols2, width), preferred_element_type=jnp.float32
        )
        re, im = z[: rows2 // 2], z[rows2 // 2 :]
        power = (re * re + im * im).reshape(RADIX, SUB, width)
        late = row + (offset + g * SUB)[None]
        inside = (late >= 0) & (late < valid)
        return jnp.maximum(best, jnp.max(jnp.where(inside, power, 0.0), 0))

    best = lax.fori_loop(
        0, groups, second_stage, jnp.zeros((SUB, width), jnp.float32), unroll=4
    )
    norm = jnp.sum(norm, 0, keepdims=True) * (SCALE * SCALE)
    out_ref[0] = jnp.max(best, 0, keepdims=True) / norm


def correlate(received, strain, starts, rows):
    parts, _, depth2, _ = received.shape
    segs = strain.shape[3]
    bins = parts * RADIX * depth2 // 2
    base, turn, second = tables(bins)
    per_tile = LANES // segs
    tiles = -(-rows // per_tile)
    width = 2 * LANES if tiles % 2 == 0 else LANES
    steps = tiles * LANES // width
    starts = jnp.tile(jnp.repeat(starts, per_tile), width // LANES)
    starts = jnp.broadcast_to(starts[None, :], (SUB, width))
    groups = 2 * bins // RADIX // SUB
    whole = pl.BlockSpec(memory_space=pltpu.VMEM)
    out = pl.pallas_call(
        functools.partial(kernel, bins),
        grid=(steps,),
        out_shape=jax.ShapeDtypeStruct((steps, 1, width), jnp.float32),
        in_specs=[whole] * 6,
        out_specs=pl.BlockSpec((1, 1, width), lambda i: (i, 0, 0)),
        scratch_shapes=[
            pltpu.VMEM(base.shape, jnp.float32),
            pltpu.VMEM((RADIX, groups * 2 * SUB, 2 * bins // RADIX), jnp.bfloat16),
            pltpu.VMEM((RADIX, parts * depth2, LANES), jnp.float32),
            pltpu.VMEM((groups, RADIX, 2 * SUB, width), jnp.bfloat16),
        ],
        compiler_params=pltpu.CompilerParams(vmem_limit_bytes=50 * 1024 * 1024),
    )(received, strain, jnp.asarray(base), jnp.asarray(turn), jnp.asarray(second), starts)
    out = out.reshape(tiles, segs, per_tile)
    return out.transpose(0, 2, 1).reshape(tiles * per_tile, segs)[:rows]


def join_parts(pieces, depth):
    if depth % SUB == 0:
        return pieces
    parts, _, _, last = pieces.shape
    pieces = pieces.reshape(parts, RADIX, 2, depth, last).transpose(1, 2, 0, 3, 4)
    return pieces.reshape(1, RADIX, 2 * parts * depth, last)


def share(piece, axes):
    count = lax.axis_size(axes)
    return lax.all_to_all(jnp.broadcast_to(piece[None], (count,) + piece.shape), axes, 0, 0, tiled=True)


def on_device(spectra, templates, valid_start):
    parts = lax.axis_size("freq")
    bins_here, _, rows_here = templates.shape
    depth = bins_here // RADIX
    rows = rows_here // parts
    bank = templates.reshape(depth, RADIX, 2, parts, rows).transpose(3, 1, 2, 0, 4)
    strain = share(spectra.reshape(bins_here * 2, -1).T, "group")
    segs = strain.shape[0] * strain.shape[1]
    strain = strain.reshape(segs, depth, RADIX, 2).transpose(2, 3, 1, 0)
    strain = jnp.broadcast_to(strain[None], (parts,) + strain.shape)
    bank = jnp.concatenate([bank, strain], 4)
    bank = jnp.pad(bank, ((0, 0),) * 4 + ((0, LANES - rows - segs),))
    bank = bank.reshape(parts, RADIX, 2 * depth, LANES)
    received = lax.all_to_all(bank, "freq", 0, 0, tiled=True)
    strain = received[..., rows : rows + segs]
    peaks = correlate(join_parts(received, depth), join_parts(strain, depth), valid_start, rows)
    peaks = share(peaks.reshape(1, -1), "freq")
    return peaks.reshape(rows_here, -1)


def solution(mesh):
    in_specs = (P("freq", None, "group"), P("freq", None, "group"), P())
    out_specs = P("group", None)
    return jax.shard_map(
        on_device, mesh=mesh, in_specs=in_specs, out_specs=out_specs, check_vma=False
    )
```
